256 devices in a mesh: seq: 64 (over x, z, core), head: 4 (over y).
Axes of the slice: x: 4, y: 4, z: 8, core: 2. Of those that a mesh axis runs over, the one named last changes fastest.
Arguments:
- q_latent: bfloat16 [16384, 1536], P('seq', 'head'), may hold values from -6 to 6
- kv_latent: bfloat16 [16384, 512], P('seq', 'head'), may hold values from -6 to 6
- k_rope: bfloat16 [16384, 64], P('seq'), may hold values from -6 to 6
- segment_ids: int32 [16384], P('seq'), may hold values from 0 to 63, as said below
- w_q_nope: bfloat16 [1536, 16384], P('seq', 'head'), may hold values from -6 to 6
- w_q_rope: bfloat16 [1536, 8192], P('seq', 'head'), may hold values from -6 to 6
- w_kv_nope: bfloat16 [512, 16384], P('seq', 'head'), may hold values from -6 to 6
- threshold: float32 [1], replicated, may hold values from 3.5 to 5.5
Outputs:
- new_q_nope: bfloat16 [1536, 16384], P('seq', 'head')
- new_q_rope: bfloat16 [1536, 8192], P('seq', 'head')
- new_kv_nope: bfloat16 [512, 16384], P('seq', 'head')
- head_max: float32 [128], P('head')
- row_max: float32 [16384, 128], P('seq', 'head')
The draws below stay inside these ranges and needn't reach their ends.
Inputs may be any that keep to these rules, and one draw needn't show every extreme that they name: segment_ids never fall along the tokens and each document has 1 to 768 tokens.
All inputs are finite; a program needn't handle non-finite values.
Results may differ from the reference program's by a relative error of at most 0.0034.
Values may be sent and summed in bfloat16 or wider, within the bound.
No kernel may reach another device: no remote copies, remote signals or barrier semaphores. Data moves between devices by JAX's collectives and lax.ppermute only.
A program may use at most 128 MiB of HBM per device.

```python
import math
import jax
import jax.numpy as jnp
from jax import lax

H = 128
D_NOPE = 128
D_ROPE = 64
QLORA = 1536
KVLORA = 512
TOK_DEV = 256
REACH = 3
TOKENS = 16384
N_SEQ = 64


def draw_segment_ids(key, part):
    count_blocks = TOKENS // TOK_DEV
    offsets = jax.random.randint(jax.random.fold_in(key, 11), (count_blocks,), 1, TOK_DEV - 1)
    position = jnp.arange(TOKENS, dtype=jnp.int32)
    block = position // TOK_DEV
    within = position % TOK_DEV
    regular = (within == offsets[block]) & (block <= count_blocks - 4)
    long_start = (count_blocks - 3) * TOK_DEV - 1
    flags = regular | (position == 0) | (position == long_start) | (position == TOKENS - 1)
    return (jnp.cumsum(flags.astype(jnp.int32)) - 1).astype(jnp.int32)


def block_scale(stream_key, shape, pieces, low, top_value):
    level, own = 1.0, jax.random.fold_in(stream_key, 6)
    for dim, parts in pieces:
        heights = jnp.exp(jax.random.uniform(jax.random.fold_in(own, dim), (parts,), jnp.float32, low / len(pieces), top_value / len(pieces)))
        level = level * jnp.repeat(heights, shape[dim] // parts).reshape([-1 if axis == dim else 1 for axis in range(len(shape))])
    return level


def gaussian(own_key, shape, scale, bound, split=(), kind=jnp.bfloat16):
    entries = jax.random.normal(own_key, shape, jnp.float32) * scale
    if len(split) > 0:
        entries = block_scale(own_key, shape, split, -0.22, 0.18) * entries
    return jnp.clip(entries, min=-bound, max=bound).astype(kind)


def setup_inputs(seed: int = 0) -> dict:
    key_list = jax.random.split(jax.random.key(seed), 9)
    q_latent = gaussian(key_list[0], (TOKENS, QLORA), 1.0, 6.0, ((0, 64), (1, 4)))
    kv_latent = gaussian(key_list[1], (TOKENS, KVLORA), 1.0, 6.0, ((0, 64), (1, 4)))
    k_rope = gaussian(key_list[2], (TOKENS, D_ROPE), 1.0, 6.0, ((0, 64),))
    segment_ids = draw_segment_ids(jax.random.fold_in(key_list[8], 71), 0)
    w_q_nope = gaussian(key_list[4], (QLORA, H * D_NOPE), 1.0, 6.0, ((0, 64), (1, 4)))
    w_q_rope = gaussian(key_list[5], (QLORA, H * D_ROPE), 1.0, 6.0, ((0, 64), (1, 4)))
    w_kv_nope = gaussian(key_list[6], (KVLORA, H * D_NOPE), 1.0, 6.0, ((0, 64), (1, 4)))
    threshold = jnp.clip(jax.random.uniform(key_list[7], (1,), jnp.float32, 3.5, 5.5), 3.5, 5.5)
    return dict(q_latent=q_latent, kv_latent=kv_latent, k_rope=k_rope, segment_ids=segment_ids, w_q_nope=w_q_nope, w_q_rope=w_q_rope, w_kv_nope=w_kv_nope, threshold=threshold)


def reference(q_latent, kv_latent, k_rope, segment_ids, w_q_nope, w_q_rope, w_kv_nope, threshold):
    q_scale = 1.0 / math.sqrt(QLORA)
    k_scale = 1.0 / math.sqrt(KVLORA)
    score_scale = 1.0 / math.sqrt(D_NOPE + D_ROPE)
    window = (REACH + 1) * TOK_DEV

    def advance(carry, block):
        old_nope, old_rope, old_seg = carry
        start = (block * TOK_DEV).astype(jnp.int32)
        q_lat = lax.dynamic_slice_in_dim(q_latent, start, TOK_DEV, 0)
        kv_lat = lax.dynamic_slice_in_dim(kv_latent, start, TOK_DEV, 0)
        rope_own = lax.dynamic_slice_in_dim(k_rope, start, TOK_DEV, 0)
        seg_own = lax.dynamic_slice_in_dim(segment_ids, start, TOK_DEV, 0)
        query_nope = (jnp.dot(q_lat, w_q_nope, preferred_element_type=jnp.float32) * q_scale).astype(jnp.bfloat16).reshape(TOK_DEV, H, D_NOPE)
        query_rope = (jnp.dot(q_lat, w_q_rope, preferred_element_type=jnp.float32) * q_scale).astype(jnp.bfloat16).reshape(TOK_DEV, H, D_ROPE)
        key_own = (jnp.dot(kv_lat, w_kv_nope, preferred_element_type=jnp.float32) * k_scale).astype(jnp.bfloat16)
        all_nope = jnp.concatenate([old_nope, key_own[None]], 0)
        all_rope = jnp.concatenate([old_rope, rope_own[None]], 0)
        all_seg = jnp.concatenate([old_seg, seg_own[None]], 0)
        keys_nope = all_nope.reshape(window, H, D_NOPE)
        keys_rope = all_rope.reshape(window, D_ROPE)
        keys_seg = all_seg.reshape(window)
        query_pos = start + jnp.arange(TOK_DEV, dtype=jnp.int32)
        key_pos = start - REACH * TOK_DEV + jnp.arange(window, dtype=jnp.int32)
        allowed = (seg_own[:, None] == keys_seg[None, :]) & (key_pos[None, :] <= query_pos[:, None]) & (key_pos[None, :] >= 0)
        nope = jnp.einsum('qhd,khd->hqk', query_nope.astype(jnp.float32), keys_nope.astype(jnp.float32))
        rope = jnp.einsum('qhd,kd->hqk', query_rope.astype(jnp.float32), keys_rope.astype(jnp.float32))
        scores = (nope + rope) * score_scale
        block_rows = lax.optimization_barrier(jnp.max(jnp.where(allowed[None], scores, jnp.float32(-1e+30)), axis=2))
        return ((all_nope[1:], all_rope[1:], all_seg[1:]), block_rows.T)
    init = (jnp.zeros((REACH, TOK_DEV, H * D_NOPE), jnp.bfloat16), jnp.zeros((REACH, TOK_DEV, D_ROPE), jnp.bfloat16), jnp.zeros((REACH, TOK_DEV), jnp.int32))
    carry, rows = lax.scan(advance, init, jnp.arange(N_SEQ, dtype=jnp.int32))
    row_max = rows.reshape(TOKENS, H)
    head_max = lax.optimization_barrier(jnp.max(row_max, axis=0))
    clip = threshold[0] / jnp.maximum(head_max, threshold[0])
    root = jnp.sqrt(clip)
    new_q_nope = (w_q_nope.astype(jnp.float32) * jnp.repeat(root, D_NOPE)[None, :]).astype(jnp.bfloat16)
    new_q_rope = (w_q_rope.astype(jnp.float32) * jnp.repeat(clip, D_ROPE)[None, :]).astype(jnp.bfloat16)
    new_kv_nope = (w_kv_nope.astype(jnp.float32) * jnp.repeat(root, D_NOPE)[None, :]).astype(jnp.bfloat16)
    return (new_q_nope, new_q_rope, new_kv_nope, head_max, row_max)
```

```python
import math

import jax
import jax.numpy as jnp
from jax import lax
from jax.experimental import pallas as pl
from jax.experimental.pallas import tpu as pltpu
from jax.sharding import Mesh
from jax.sharding import PartitionSpec as P

D_NOPE = 128
D_ROPE = 64
QLORA = 1536
KVLORA = 512
BLK = 256
HEADS = 8
NX = 4
Q_COLS = HEADS * (D_NOPE + D_ROPE)
W_COLS = 3 * Q_COLS + HEADS * D_NOPE
NEG = -1e30
SEQ = ("x", "z", "c")


def place_of(block, shift=0):
    group, i = divmod(block, 4)
    group = (group + shift) % 16
    xo, zh = divmod(group, 4)
    x, z, c = (i + xo) % 4, zh * 2 + (xo & 1), xo >> 1
    return (x * 8 + z) * 2 + c


OWN_ROUTE = [(b, place_of(b)) for b in range(64)]
HALO_ROUTE = [(b, place_of(b, 1)) for b in range(60) if b % 4]


def home_route(slot):
    route = []
    for b in range(64):
        xzc = place_of(b)
        x, zc = divmod(xzc, 16)
        route.append((((x + slot) % 4) * 16 + zc, b))
    return route


HOME_ROUTES = [home_route(d) for d in range(4)]


def ring(value, axis, distance):
    n = lax.axis_size(axis)
    return lax.ppermute(value, axis, [(i, (i + distance) % n) for i in range(n)])


def pack_weights_kernel(x_ref, wn_ref, wr_ref, wk_ref, *out_refs):
    for d in range(4):
        to = lax.rem(x_ref[0] + d, 4)
        out = out_refs[d]
        for t in range(3):
            rows = pl.ds(t * 8, 8)
            at = t * Q_COLS
            out[:, at : at + 1024] = wn_ref[rows, pl.ds(pl.multiple_of(to * 1024, 1024), 1024)]
            out[:, at + 1024 : at + 1536] = wr_ref[rows, pl.ds(pl.multiple_of(to * 512, 512), 512)]
        out[:, 3 * Q_COLS :] = wk_ref[:, pl.ds(pl.multiple_of(to * 1024, 1024), 1024)]


def pack_weights(x, wn, wr, wk):
    vmem = pl.BlockSpec(memory_space=pltpu.VMEM)
    return pl.pallas_call(
        pack_weights_kernel,
        out_shape=[jax.ShapeDtypeStruct((8, W_COLS), jnp.bfloat16)] * 4,
        in_specs=[pl.BlockSpec(memory_space=pltpu.SMEM), vmem, vmem, vmem],
        out_specs=[vmem] * 4,
        name="pack_weights",
    )(x, wn, wr, wk)


def pack_latents_kernel(q_ref, kv_ref, rope_ref, seg_ref, own_ref, halo_ref):
    old = lax.broadcasted_iota(jnp.int32, (384, 384), 0)
    new = lax.broadcasted_iota(jnp.int32, (384, 384), 1)
    t, rest = new // 128, new % 128
    pick = old == (rest // 8) * 24 + t * 8 + rest % 8
    chosen = jnp.where(pick, 1.0, 0.0).astype(jnp.bfloat16)
    own_ref[:, :384] = jnp.dot(q_ref[...], chosen, preferred_element_type=jnp.float32).astype(
        jnp.bfloat16
    )
    kv = kv_ref[...]
    own_ref[:, 384:512] = kv
    halo_ref[:, :128] = kv
    seg = jnp.broadcast_to((seg_ref[...] + 1).astype(jnp.float32), (128, BLK))
    column = jnp.transpose(seg).astype(jnp.bfloat16)
    rope = rope_ref[...]
    for ref, at in ((own_ref, 512), (halo_ref, 128)):
        ref[:, at : at + 128] = column
        ref[:, at : at + 64] = rope


def pack_latents(q, kv, rope, seg):
    vmem = pl.BlockSpec(memory_space=pltpu.VMEM)
    return pl.pallas_call(
        pack_latents_kernel,
        out_shape=[
            jax.ShapeDtypeStruct((BLK, 640), jnp.bfloat16),
            jax.ShapeDtypeStruct((BLK, 256), jnp.bfloat16),
        ],
        in_specs=[vmem] * 4,
        out_specs=[vmem] * 2,
        name="pack_latents",
    )(q, kv, rope, seg.reshape(1, BLK))


def main_kernel(
    place_ref, w_ref, ql_ref, kv_ref, rs_ref, rm_ref, hm_ref,
    wn, wr, wk, kn, kr, qn, qr, bias, sems,
):
    i_own, delta = place_ref[0], place_ref[1]
    copies = []
    for e in range(4):
        slot = lax.rem(delta + e, 4)
        copies.append(
            pltpu.make_async_copy(
                w_ref.at[slot, :, pl.ds(3 * Q_COLS, 1024)], wk.at[pl.ds(e * 128, 128), :], sems.at[e]
            )
        )
    for e in range(4):
        slot = lax.rem(delta + e, 4)
        for t in range(3):
            rows = pl.ds((e * 3 + t) * 128, 128)
            n = 4 + 2 * (e * 3 + t)
            copies.append(
                pltpu.make_async_copy(
                    w_ref.at[slot, :, pl.ds(t * Q_COLS, 1024)], wn.at[rows, :], sems.at[n]
                )
            )
            copies.append(
                pltpu.make_async_copy(
                    w_ref.at[slot, :, pl.ds(t * Q_COLS + 1024, 512)], wr.at[rows, :], sems.at[n + 1]
                )
            )
    for copy in copies:
        copy.start()

    lane = lax.broadcasted_iota(jnp.int32, (BLK, 128), 1)
    seg_rows = []
    for d in range(8):
        rs = rs_ref[pl.ds(d * BLK, BLK), :].astype(jnp.float32)
        kr[0, d] = jnp.where(lane < 64, rs, 0.0).astype(jnp.bfloat16)
        kr[1, d] = jnp.where(lane >= 64, pltpu.roll(rs, 64, 1), 0.0).astype(jnp.bfloat16)
        if d < 4:
            seg_rows.append(jnp.transpose(rs)[64:65, :])
    k_iota = lax.broadcasted_iota(jnp.int32, (BLK, BLK), 0)
    q_iota = lax.broadcasted_iota(jnp.int32, (BLK, BLK), 1)
    which = []
    for d in range(4):
        i_q = lax.rem(i_own - d + 4, 4)
        for f in range(4):
            i_k = lax.rem(i_own - f + 4, 4)
            at = jnp.where(i_k > i_q, f + 4, f)
            which.append(at)
            seg_k = rs_ref[pl.ds(pl.multiple_of(at * BLK, BLK), BLK), 64:65].astype(jnp.float32)
            allowed = seg_k == seg_rows[d]
            if d == f:
                allowed = allowed & (k_iota <= q_iota)
            bias[d, f] = jnp.where(allowed, 0.0, NEG)

    for copy in copies[:4]:
        copy.wait()
    k_scale = 1.0 / math.sqrt(KVLORA)
    for b in range(8):
        kv = kv_ref[pl.ds(b * BLK, BLK), :]
        kn[b] = (jnp.dot(kv, wk[...], preferred_element_type=jnp.float32) * k_scale).astype(
            jnp.bfloat16
        )
    for copy in copies[4:]:
        copy.wait()
    q_scale = 1.0 / math.sqrt(QLORA)
    for d in range(4):
        ql = ql_ref[pl.ds(d * BLK, BLK), :]
        qn[d] = (jnp.dot(ql, wn[...], preferred_element_type=jnp.float32) * q_scale).astype(
            jnp.bfloat16
        )
        qr[d] = (jnp.dot(ql, wr[...], preferred_element_type=jnp.float32) * q_scale).astype(
            jnp.bfloat16
        )

    score_scale = 1.0 / math.sqrt(D_NOPE + D_ROPE)
    head_best = []
    for h in range(HEADS):
        best_h = None
        for d in range(4):
            query = jnp.concatenate(
                [qn[d, :, h * 128 : h * 128 + 128], qr[d, :, (h // 2) * 128 : (h // 2) * 128 + 128]],
                axis=1,
            )
            best = None
            for f in range(4):
                at = which[d * 4 + f]
                keys = jnp.concatenate([kn[at, :, h * 128 : h * 128 + 128], kr[h % 2, at]], axis=1)
                s = lax.dot_general(
                    keys, query, (((1,), (1,)), ((), ())), preferred_element_type=jnp.float32
                )
                s = jnp.max((s + bias[d, f]).reshape(BLK // 8, 8, BLK), axis=0)
                best = s if best is None else jnp.maximum(best, s)
            row = jnp.max(best, axis=0, keepdims=True) * score_scale
            rm_ref[d, h : h + 1, :] = row
            best_h = row if best_h is None else jnp.maximum(best_h, row)
        head_best.append(jnp.max(best_h, axis=1, keepdims=True))
    hm_lane = lax.broadcasted_iota(jnp.int32, (1, 128), 1)
    line = jnp.zeros((1, 128), jnp.float32)
    for h in range(HEADS):
        line = jnp.where(hm_lane == h, head_best[h], line)
    hm_ref[...] = jnp.broadcast_to(line, hm_ref.shape)


def main(place, w, ql, kv, rs):
    vmem = pl.BlockSpec(memory_space=pltpu.VMEM)
    bf16, f32 = jnp.bfloat16, jnp.float32
    return pl.pallas_call(
        main_kernel,
        out_shape=[
            jax.ShapeDtypeStruct((4, HEADS, BLK), f32),
            jax.ShapeDtypeStruct((64, 128), f32),
        ],
        in_specs=[
            pl.BlockSpec(memory_space=pltpu.SMEM),
            pl.BlockSpec(memory_space=pl.ANY),
            vmem,
            vmem,
            vmem,
        ],
        out_specs=[vmem, vmem],
        scratch_shapes=[
            pltpu.VMEM((QLORA, 1024), bf16),
            pltpu.VMEM((QLORA, 512), bf16),
            pltpu.VMEM((KVLORA, 1024), bf16),
            pltpu.VMEM((8, BLK, 1024), bf16),
            pltpu.VMEM((2, 8, BLK, 128), bf16),
            pltpu.VMEM((4, BLK, 1024), bf16),
            pltpu.VMEM((4, BLK, 512), bf16),
            pltpu.VMEM((4, 4, BLK, BLK), f32),
            pltpu.SemaphoreType.DMA((28,)),
        ],
        compiler_params=pltpu.CompilerParams(vmem_limit_bytes=48 * 2**20),
        cost_estimate=pl.CostEstimate(
            flops=2 * 2048 * 512 * 1024 + 2 * 1024 * 1536 * 1536 + 2 * 128 * 256**3,
            bytes_accessed=12 * 2**20,
            transcendentals=0,
        ),
        name="row_maxima",
    )(place, w, ql, kv, rs)


def gathered_weights(wn, wr, wk):
    x = lax.axis_index("x")
    parts = pack_weights(x.reshape(1).astype(jnp.int32), wn, wr, wk)
    moved = [parts[0], ring(parts[1], "x", 1), ring(parts[2], "x", 2), ring(parts[3], "x", -1)]
    return lax.all_gather(jnp.stack(moved), ("z", "c"), axis=1, tiled=True)


def gathered_latents(q_latent, kv_latent, k_rope, segment_ids):
    own, halo = pack_latents(q_latent, kv_latent, k_rope, segment_ids)
    own = lax.ppermute(own, SEQ, OWN_ROUTE)
    halo = lax.ppermute(halo, SEQ, HALO_ROUTE)
    first = jnp.concatenate([own[:128, :512], halo[:128, :128]], axis=1)
    rest = [
        own[128:, :512], halo[128:, :128],
        own[:128, 512:], halo[:128, 128:], own[128:, 512:], halo[128:, 128:],
    ]
    rest = jnp.concatenate(rest, axis=1)
    by_y = [first, ring(first, "y", 1), ring(first, "y", 2), ring(first, "y", -1)]
    by_x = [rest, ring(rest, "x", 1), ring(rest, "x", 2), ring(rest, "x", -1)]
    by_y = jnp.stack(by_y)
    far = jnp.stack([r[:, :640] for r in by_x])

    def both_ways(value, axis):
        up, down = ring(value, axis, 1), ring(value, axis, -1)
        two = [ring(up[:2], axis, 1), ring(down[2:], axis, -1)]
        return [list(value), list(up), list(two[0]) + list(two[1]), list(down)]

    a = both_ways(by_y, "x")
    b = both_ways(far, "y")
    ql, kv_own, kv_halo = [], [], []
    for d in range(4):
        ra = jnp.concatenate
        ql.append(ra([a[d][e][:, :384] for e in range(4)], axis=1))
        ql.append(ra([b[e][d][:, :384] for e in range(4)], axis=1))
        kv_own.append(ra([a[d][e][:, 384:512] for e in range(4)], axis=1))
        kv_own.append(ra([b[e][d][:, 384:512] for e in range(4)], axis=1))
        kv_halo.append(ra([a[d][e][:, 512:] for e in range(4)], axis=1))
        kv_halo.append(ra([b[e][d][:, 512:] for e in range(4)], axis=1))
    ql = jnp.concatenate(ql, axis=0)
    kv = jnp.concatenate(kv_own + kv_halo, axis=0)
    rs = [r[:, at : at + 128] for r in by_x for at in (640, 896)]
    rs += [r[:, at : at + 128] for r in by_x for at in (768, 1024)]
    return ql, kv, jnp.concatenate(rs, axis=0)


def local(q_latent, kv_latent, k_rope, segment_ids, w_q_nope, w_q_rope, w_kv_nope, threshold):
    x, z, c, y = (lax.axis_index(a).astype(jnp.int32) for a in ("x", "z", "c", "y"))
    w = gathered_weights(w_q_nope, w_q_rope, w_kv_nope)
    ql, kv, rs = gathered_latents(q_latent, kv_latent, k_rope, segment_ids)
    xo = lax.rem(z, 2) + 2 * c
    place = jnp.stack([lax.rem(x - xo + 4, 4), lax.rem(x - y + 4, 4)])
    rm, hm = main(place, w, ql, kv, rs)

    everything = lax.all_to_all(hm, SEQ, 0, 0, tiled=True)
    head_max = jnp.max(everything.reshape(4, 16, 128), axis=1)[:, :HEADS].reshape(32)
    back = [lax.ppermute(rm[d], SEQ, HOME_ROUTES[d]) for d in range(4)]
    first = lax.rem(lax.rem(z, 2) * 2 + c + x, 4)
    twice = jnp.concatenate(back + back[:3], axis=0)
    row_max = lax.dynamic_slice_in_dim(twice, 8 * lax.rem(4 - first, 4), 32, axis=0).T

    clip = threshold[0] / jnp.maximum(head_max, threshold[0])
    root = jnp.sqrt(clip)
    new_q_nope = (w_q_nope.astype(jnp.float32) * jnp.repeat(root, D_NOPE)[None, :]).astype(
        jnp.bfloat16
    )
    new_q_rope = (w_q_rope.astype(jnp.float32) * jnp.repeat(clip, D_ROPE)[None, :]).astype(
        jnp.bfloat16
    )
    new_kv_nope = (w_kv_nope.astype(jnp.float32) * jnp.repeat(root, D_NOPE)[None, :]).astype(
        jnp.bfloat16
    )
    return (new_q_nope, new_q_rope, new_kv_nope, head_max, row_max)


def solution(mesh):
    fine = Mesh(mesh.devices.reshape(4, 8, 2, 4), ("x", "z", "c", "y"))
    in_specs = (
        P(SEQ, "y"),
        P(SEQ, "y"),
        P(SEQ, None),
        P(SEQ),
        P(SEQ, "y"),
        P(SEQ, "y"),
        P(SEQ, "y"),
        P(),
    )
    out_specs = (P(SEQ, "y"), P(SEQ, "y"), P(SEQ, "y"), P("y"), P(SEQ, "y"))
    return jax.shard_map(local, mesh=fine, in_specs=in_specs, out_specs=out_specs, check_vma=False)
```

```python
import math

import jax
import jax.numpy as jnp
from jax import lax
from jax.experimental import pallas as pl
from jax.experimental.pallas import tpu as pltpu
from jax.sharding import Mesh
from jax.sharding import PartitionSpec as P

D_NOPE = 128
D_ROPE = 64
QLORA = 1536
KVLORA = 512
BLK = 256
HEADS = 8
NX = 4
Q_COLS = HEADS * (D_NOPE + D_ROPE)
W_COLS = 3 * Q_COLS + HEADS * D_NOPE
NEG = -1e30
SEQ = ("x", "zh", "zl", "c")


def place_of(block, shift=0):
    group, i = divmod(block, 4)
    group = (group + shift) % 16
    xo, zh = divmod(group, 4)
    x, z, c = (i + xo) % 4, zh * 2 + (xo & 1), xo >> 1
    return (x * 8 + z) * 2 + c


OWN_ROUTE = [(b, place_of(b)) for b in range(64)]
HALO_ROUTE = [(b, place_of(b, 1)) for b in range(60) if b % 4]
Z_ROUTE = [(z * 2 + c, (z + (-1 if c else 1)) % 8 * 2 + c) for z in range(8) for c in range(2)]


def ring(value, axis, distance):
    n = lax.axis_size(axis)
    return lax.ppermute(value, axis, [(i, (i + distance) % n) for i in range(n)])


def pack_weights_kernel(x_ref, wn_ref, wr_ref, wk_ref, *out_refs):
    for d in range(4):
        to = lax.rem(x_ref[0] + d, 4)
        out = out_refs[d]
        for t in range(3):
            rows = pl.ds(t * 8, 8)
            at = t * Q_COLS
            out[:, at : at + 1024] = wn_ref[rows, pl.ds(pl.multiple_of(to * 1024, 1024), 1024)]
            out[:, at + 1024 : at + 1536] = wr_ref[rows, pl.ds(pl.multiple_of(to * 512, 512), 512)]
        out[:, 3 * Q_COLS :] = wk_ref[:, pl.ds(pl.multiple_of(to * 1024, 1024), 1024)]


def pack_weights(x, wn, wr, wk):
    vmem = pl.BlockSpec(memory_space=pltpu.VMEM)
    return pl.pallas_call(
        pack_weights_kernel,
        out_shape=[jax.ShapeDtypeStruct((8, W_COLS), jnp.bfloat16)] * 4,
        in_specs=[pl.BlockSpec(memory_space=pltpu.SMEM), vmem, vmem, vmem],
        out_specs=[vmem] * 4,
        name="pack_weights",
    )(x, wn, wr, wk)


def pack_latents_kernel(q_ref, kv_ref, rope_ref, seg_ref, own_ref, halo_ref):
    old = lax.broadcasted_iota(jnp.int32, (384, 384), 0)
    new = lax.broadcasted_iota(jnp.int32, (384, 384), 1)
    t, rest = new // 128, new % 128
    pick = old == (rest // 8) * 24 + t * 8 + rest % 8
    chosen = jnp.where(pick, 1.0, 0.0).astype(jnp.bfloat16)
    own_ref[:, :384] = jnp.dot(q_ref[...], chosen, preferred_element_type=jnp.float32).astype(
        jnp.bfloat16
    )
    kv = kv_ref[...]
    own_ref[:, 384:512] = kv
    halo_ref[:, :128] = kv
    seg = jnp.broadcast_to((seg_ref[...] + 1).astype(jnp.float32), (128, BLK))
    column = jnp.transpose(seg).astype(jnp.bfloat16)
    rope = jnp.transpose(rope_ref[...].astype(jnp.float32)).astype(jnp.bfloat16)
    for ref, at in ((own_ref, 512), (halo_ref, 128)):
        ref[:, at : at + 128] = column
        ref[:, at : at + 64] = rope


def pack_latents(q, kv, rope, seg):
    vmem = pl.BlockSpec(memory_space=pltpu.VMEM)
    return pl.pallas_call(
        pack_latents_kernel,
        out_shape=[
            jax.ShapeDtypeStruct((BLK, 640), jnp.bfloat16),
            jax.ShapeDtypeStruct((BLK, 256), jnp.bfloat16),
        ],
        in_specs=[vmem] * 4,
        out_specs=[vmem] * 2,
        name="pack_latents",
    )(q, kv, rope.T, seg.reshape(1, BLK))


def join_kernel(c_ref, mine_ref, theirs_ref, out_ref):
    for core in range(2):

        @pl.when(c_ref[0] == core)
        def _():
            out_ref[:, core * 8 : core * 8 + 8, :] = mine_ref[...]
            out_ref[:, 8 - core * 8 : 16 - core * 8, :] = theirs_ref[...]


def join(c, mine, theirs):
    vmem = pl.BlockSpec(memory_space=pltpu.VMEM)
    return pl.pallas_call(
        join_kernel,
        out_shape=jax.ShapeDtypeStruct((4, 16, W_COLS), jnp.bfloat16),
        in_specs=[pl.BlockSpec(memory_space=pltpu.SMEM), vmem, vmem],
        out_specs=vmem,
        name="join_cores",
    )(c.reshape(1), mine, theirs)


N_W, N_L, N_R = 9, 5, 4


def main_kernel(place_ref, *refs):
    w_refs, refs = refs[:N_W], refs[N_W:]
    a_refs, b_refs, r_refs = refs[:N_L], refs[N_L : 2 * N_L], refs[2 * N_L : 2 * N_L + N_R]
    ex_ref, w, lat, rs, kn, kr, qn, qr, bias, sems = refs[2 * N_L + N_R :]
    i_own, delta, xo, z, c = (place_ref[n] for n in range(5))
    count = [0]

    def fetch(src, dst):
        copy = pltpu.make_async_copy(src, dst, sems.at[count[0]])
        count[0] += 1
        copy.start()
        return copy

    sign = 2 * c - 1
    early = [fetch(r_refs[d], rs.at[d]) for d in range(4)]
    late = []
    for n in range(N_W):
        step = (n + 1) // 2
        towards = sign if n % 2 else -sign
        rows = pl.ds(pl.multiple_of(lax.rem(z + towards * step + 8, 8) * 16, 16), 16)
        if step < 4:
            late.append(fetch(w_refs[n], w.at[:, rows, :]))
        else:
            half = pl.ds(2 * c, 2) if n % 2 else pl.ds(2 - 2 * c, 2)
            late.append(fetch(w_refs[n], w.at[half, rows, :]))
    low, high = pl.ds(0, 128), pl.ds(128, 128)
    for n, d in enumerate((0, 1, 3)):
        late.append(fetch(a_refs[n], lat.at[d, :, low, :]))
        late.append(fetch(b_refs[n], lat.at[:, d, high, :]))
    for n in range(2):
        late.append(fetch(a_refs[3 + n], lat.at[2, pl.ds(2 * n, 2), low, :]))
        late.append(fetch(b_refs[3 + n], lat.at[pl.ds(2 * n, 2), 2, high, :]))

    for copy in early:
        copy.wait()
    lane = lax.broadcasted_iota(jnp.int32, (128, 128), 1)
    seg_rows = []
    for d in range(4):
        seg_row = []
        for n in range(4):
            at = d + 4 * (n % 2)
            rows = pl.ds((n // 2) * 128, 128)
            part = rs[d, :, n * 128 : n * 128 + 128].astype(jnp.float32)
            kr[0, at, rows, :] = jnp.where(lane < 64, part, 0.0).astype(jnp.bfloat16)
            turned = pltpu.roll(part, 64, 1)
            kr[1, at, rows, :] = jnp.where(lane >= 64, turned, 0.0).astype(jnp.bfloat16)
            kr[2, at, rows, :] = turned.astype(jnp.bfloat16)
            if n % 2 == 0:
                seg_row.append(jnp.transpose(part)[64:65, :])
        seg_rows.append(jnp.concatenate(seg_row, axis=1))
    k_iota = lax.broadcasted_iota(jnp.int32, (BLK, BLK), 0)
    q_iota = lax.broadcasted_iota(jnp.int32, (BLK, BLK), 1)
    which = []
    for d in range(4):
        i_q = lax.rem(i_own - d + 4, 4)
        for f in range(4):
            i_k = lax.rem(i_own - f + 4, 4)
            at = jnp.where(i_k > i_q, f + 4, f)
            which.append(at)
            seg_k = kr[2, at, :, 0:1].astype(jnp.float32)
            allowed = seg_k == seg_rows[d]
            if d == f:
                allowed = allowed & (k_iota <= q_iota)
            bias[d, f] = jnp.where(allowed, 0.0, NEG)

    for copy in late:
        copy.wait()
    slots = [lax.rem(delta + e, 4) for e in range(4)]
    k_scale = 1.0 / math.sqrt(KVLORA)
    wk = jnp.concatenate([w[slot, :, 3 * Q_COLS :] for slot in slots], axis=0)
    for b in range(8):
        at = 384 + 128 * (b // 4)
        kv = jnp.concatenate([lat[b % 4, e, :, at : at + 128] for e in range(4)], axis=1)
        kn[b] = (jnp.dot(kv, wk, preferred_element_type=jnp.float32) * k_scale).astype(jnp.bfloat16)
    q_scale = 1.0 / math.sqrt(QLORA)
    for out, at, columns in ((qn, 0, 512), (qn, 512, 512), (qr, 1024, 512)):
        wq = [
            w[slot, :, t * Q_COLS + at : t * Q_COLS + at + columns]
            for slot in slots
            for t in range(3)
        ]
        wq = jnp.concatenate(wq, axis=0)
        for d in range(4):
            ql = jnp.concatenate([lat[d, e, :, :384] for e in range(4)], axis=1)
            to = at % 1024
            out[d, :, to : to + columns] = (
                jnp.dot(ql, wq, preferred_element_type=jnp.float32) * q_scale
            ).astype(jnp.bfloat16)

    score_scale = 1.0 / math.sqrt(D_NOPE + D_ROPE)
    for h in range(HEADS):
        best_h = None
        for d in range(4):
            pair = (h // 2) * 128
            query = jnp.concatenate(
                [qn[d, :, h * 128 : h * 128 + 128], qr[d, :, pair : pair + 128]], axis=1
            )
            best = None
            for f in range(4):
                at = which[d * 4 + f]
                keys = jnp.concatenate([kn[at, :, h * 128 : h * 128 + 128], kr[h % 2, at]], axis=1)
                s = lax.dot_general(
                    keys, query, (((1,), (1,)), ((), ())), preferred_element_type=jnp.float32
                )
                s = jnp.max((s + bias[d, f]).reshape(BLK // 8, 8, BLK), axis=0)
                best = s if best is None else jnp.maximum(best, s)
            row = jnp.max(best, axis=0, keepdims=True) * score_scale
            home = 4 * xo + lax.rem(i_own - d + 4, 4)
            ex_ref[home, h : h + 1, 0:BLK] = row
            best_h = row if best_h is None else jnp.maximum(best_h, row)
        top = jnp.max(best_h, axis=1, keepdims=True)
        ex_ref[0, h : h + 1, BLK:] = jnp.broadcast_to(top, (1, 128))
    tops = ex_ref[0, :, BLK:]
    for n in range(1, 16):
        ex_ref[n, :, BLK:] = tops


def main(place, w, a, b, r):
    vmem = pl.BlockSpec(memory_space=pltpu.VMEM)
    bf16, f32 = jnp.bfloat16, jnp.float32
    return pl.pallas_call(
        main_kernel,
        out_shape=jax.ShapeDtypeStruct((16, HEADS, BLK + 128), f32),
        in_specs=[pl.BlockSpec(memory_space=pltpu.SMEM)]
        + [pl.BlockSpec(memory_space=pl.ANY)] * (N_W + 2 * N_L + N_R),
        out_specs=vmem,
        scratch_shapes=[
            pltpu.VMEM((4, 128, W_COLS), bf16),
            pltpu.VMEM((4, 4, BLK, 640), bf16),
            pltpu.VMEM((4, 128, 512), bf16),
            pltpu.VMEM((8, BLK, 1024), bf16),
            pltpu.VMEM((3, 8, BLK, 128), bf16),
            pltpu.VMEM((4, BLK, 1024), bf16),
            pltpu.VMEM((4, BLK, 512), bf16),
            pltpu.VMEM((4, 4, BLK, BLK), f32),
            pltpu.SemaphoreType.DMA((N_W + 2 * N_L + N_R,)),
        ],
        compiler_params=pltpu.CompilerParams(vmem_limit_bytes=48 * 2**20),
        cost_estimate=pl.CostEstimate(
            flops=2 * 2048 * 512 * 1024 + 2 * 1024 * 1536 * 1536 + 2 * 128 * 256**3,
            bytes_accessed=12 * 2**20,
            transcendentals=0,
        ),
        name="row_maxima",
    )(place, *w, *a, *b, *r)


def exchanged_weights(x, c, wn, wr, wk):
    parts = pack_weights(x.reshape(1), wn, wr, wk)
    moved = [parts[0], ring(parts[1], "x", 1), ring(parts[2], "x", 2), ring(parts[3], "x", -1)]
    mine = jnp.stack(moved)
    return join(c, mine, ring(mine, "c", 1))


def gathered_weights(c, own):
    pieces = [own]
    held = own
    for step in range(1, 5):
        if step == 4:
            held = lax.dynamic_slice_in_dim(held, 2 * c, 2, axis=0)
        held = lax.ppermute(held, ("zh", "zl", "c"), Z_ROUTE)
        pieces += [held, ring(held, "c", 1)]
    return pieces


def gathered_latents(q_latent, kv_latent, k_rope, segment_ids):
    own, halo = pack_latents(q_latent, kv_latent, k_rope, segment_ids)
    own = lax.ppermute(own, SEQ, OWN_ROUTE)
    halo = lax.ppermute(halo, SEQ, HALO_ROUTE)
    first = jnp.concatenate([own[:128, :512], halo[:128, :128]], axis=1)
    second = jnp.concatenate([own[128:, :512], halo[128:, :128]], axis=1)
    ropes = [own[:128, 512:], halo[:128, 128:], own[128:, 512:], halo[128:, 128:]]
    ropes = jnp.concatenate(ropes, axis=1)

    def around(value, axis):
        return [value, ring(value, axis, 1), ring(value, axis, 2), ring(value, axis, -1)]

    def both_ways(value, axis):
        up, down = ring(value, axis, 1), ring(value, axis, -1)
        return [value, up, down, ring(up[:2], axis, 1), ring(down[2:], axis, -1)]

    by_y, by_x, r = around(first, "y"), around(second, "x"), around(ropes, "x")
    return both_ways(jnp.stack(by_y), "x"), both_ways(jnp.stack(by_x), "y"), r


def local(q_latent, kv_latent, k_rope, segment_ids, w_q_nope, w_q_rope, w_kv_nope, threshold):
    x, zh, zl, c, y = (lax.axis_index(a).astype(jnp.int32) for a in ("x", "zh", "zl", "c", "y"))
    own = exchanged_weights(x, c, w_q_nope, w_q_rope, w_kv_nope)
    w = gathered_weights(c, own)
    a, b, r = gathered_latents(q_latent, kv_latent, k_rope, segment_ids)
    xo = zl + 2 * c
    place = jnp.stack([lax.rem(x - xo + 4, 4), lax.rem(x - y + 4, 4), xo, 2 * zh + zl, c])
    out = main(place, w, a, b, r)

    got = lax.all_to_all(out, ("x", "zl", "c"), 0, 0, tiled=True)
    got = got.reshape(4, 4, HEADS, BLK + 128)
    top = jnp.max(got[..., BLK:], axis=1).reshape(4 * HEADS, 128)
    top = jnp.maximum(
        jnp.maximum(top, ring(top, "zh", 2)), jnp.maximum(ring(top, "zh", 1), ring(top, "zh", -1))
    )
    head_max = top[:, 0]
    sent_from = 2 * lax.rem(x, 2) + x // 2
    rows = lax.dynamic_slice_in_dim(got[..., :BLK], sent_from, 1, axis=1)
    row_max = rows.reshape(4 * HEADS, BLK).T

    clip = threshold[0] / jnp.maximum(head_max, threshold[0])
    root = jnp.sqrt(clip)
    new_q_nope = (w_q_nope.astype(jnp.float32) * jnp.repeat(root, D_NOPE)[None, :]).astype(
        jnp.bfloat16
    )
    new_q_rope = (w_q_rope.astype(jnp.float32) * jnp.repeat(clip, D_ROPE)[None, :]).astype(
        jnp.bfloat16
    )
    new_kv_nope = (w_kv_nope.astype(jnp.float32) * jnp.repeat(root, D_NOPE)[None, :]).astype(
        jnp.bfloat16
    )
    return (new_q_nope, new_q_rope, new_kv_nope, head_max, row_max)


def solution(mesh):
    fine = Mesh(mesh.devices.reshape(4, 4, 2, 2, 4), ("x", "zh", "zl", "c", "y"))
    in_specs = (
        P(SEQ, "y"),
        P(SEQ, "y"),
        P(SEQ, None),
        P(SEQ),
        P(SEQ, "y"),
        P(SEQ, "y"),
        P(SEQ, "y"),
        P(),
    )
    out_specs = (P(SEQ, "y"), P(SEQ, "y"), P(SEQ, "y"), P("y"), P(SEQ, "y"))
    return jax.shard_map(local, mesh=fine, in_specs=in_specs, out_specs=out_specs, check_vma=False)
```

```python
import math

import jax
import jax.numpy as jnp
from jax import lax
from jax.experimental import pallas as pl
from jax.experimental.pallas import tpu as pltpu
from jax.sharding import Mesh
from jax.sharding import PartitionSpec as P

D_NOPE = 128
D_ROPE = 64
QLORA = 1536
KVLORA = 512
BLK = 256
HEADS = 8
NX = 4
Q_COLS = HEADS * (D_NOPE + D_ROPE)
W_COLS = 3 * Q_COLS + HEADS * D_NOPE
NEG = -1e30
SEQ = ("x", "zh", "zl", "c")


def place_of(block, shift=0):
    group, i = divmod(block, 4)
    group = (group + shift) % 16
    xo, zh = divmod(group, 4)
    x, z, c = (i + xo) % 4, zh * 2 + (xo & 1), xo >> 1
    return (x * 8 + z) * 2 + c


OWN_ROUTE = [(b, place_of(b)) for b in range(64)]
HALO_ROUTE = [(b, place_of(b, 1)) for b in range(60) if b % 4]
Z_ROUTE = [(z * 2 + c, (z + (-1 if c else 1)) % 8 * 2 + c) for z in range(8) for c in range(2)]

TURNS = ((1, 3), (3, 1))
X_ROUTES = [[(x * 2 + c, (x ^ TURNS[c][n]) * 2 + c) for x in range(4) for c in range(2)] for n in range(2)]
Y_ROUTES = [[(c * 4 + y, c * 4 + (y ^ TURNS[c][n])) for y in range(4) for c in range(2)] for n in range(2)]


def ring(value, axis, distance):
    n = lax.axis_size(axis)
    return lax.ppermute(value, axis, [(i, (i + distance) % n) for i in range(n)])


def pack_weights_kernel(x_ref, wn_ref, wr_ref, wk_ref, *out_refs):
    for d in range(4):
        to = lax.rem(x_ref[0] + d, 4)
        out = out_refs[d]
        for t in range(3):
            rows = pl.ds(t * 8, 8)
            at = t * Q_COLS
            out[:, at : at + 1024] = wn_ref[rows, pl.ds(pl.multiple_of(to * 1024, 1024), 1024)]
            out[:, at + 1024 : at + 1536] = wr_ref[rows, pl.ds(pl.multiple_of(to * 512, 512), 512)]
        out[:, 3 * Q_COLS :] = wk_ref[:, pl.ds(pl.multiple_of(to * 1024, 1024), 1024)]


def pack_weights(x, wn, wr, wk):
    vmem = pl.BlockSpec(memory_space=pltpu.VMEM)
    return pl.pallas_call(
        pack_weights_kernel,
        out_shape=[jax.ShapeDtypeStruct((8, W_COLS), jnp.bfloat16)] * 4,
        in_specs=[pl.BlockSpec(memory_space=pltpu.SMEM), vmem, vmem, vmem],
        out_specs=[vmem] * 4,
        name="pack_weights",
    )(x, wn, wr, wk)


def pack_latents_kernel(q_ref, kv_ref, rope_ref, seg_ref, own_ref, halo_ref):
    old = lax.broadcasted_iota(jnp.int32, (384, 384), 0)
    new = lax.broadcasted_iota(jnp.int32, (384, 384), 1)
    t, rest = new // 128, new % 128
    pick = old == (rest // 8) * 24 + t * 8 + rest % 8
    chosen = jnp.where(pick, 1.0, 0.0).astype(jnp.bfloat16)
    own_ref[:, :384] = jnp.dot(q_ref[...], chosen, preferred_element_type=jnp.float32).astype(
        jnp.bfloat16
    )
    kv = kv_ref[...]
    own_ref[:, 384:512] = kv
    halo_ref[:, :128] = kv
    seg = jnp.broadcast_to((seg_ref[...] + 1).astype(jnp.float32), (128, BLK))
    column = jnp.transpose(seg).astype(jnp.bfloat16)
    rope = jnp.transpose(rope_ref[...].astype(jnp.float32)).astype(jnp.bfloat16)
    for ref, at in ((own_ref, 512), (halo_ref, 128)):
        ref[:, at : at + 128] = column
        ref[:, at : at + 64] = rope


def pack_latents(q, kv, rope, seg):
    vmem = pl.BlockSpec(memory_space=pltpu.VMEM)
    return pl.pallas_call(
        pack_latents_kernel,
        out_shape=[
            jax.ShapeDtypeStruct((BLK, 640), jnp.bfloat16),
            jax.ShapeDtypeStruct((BLK, 256), jnp.bfloat16),
        ],
        in_specs=[vmem] * 4,
        out_specs=[vmem] * 2,
        name="pack_latents",
    )(q, kv, rope.T, seg.reshape(1, BLK))


def join_kernel(c_ref, mine_ref, theirs_ref, out_ref):
    for core in range(2):

        @pl.when(c_ref[0] == core)
        def _():
            out_ref[:, core * 8 : core * 8 + 8, :] = mine_ref[...]
            out_ref[:, 8 - core * 8 : 16 - core * 8, :] = theirs_ref[...]


def join(c, mine, theirs):
    vmem = pl.BlockSpec(memory_space=pltpu.VMEM)
    return pl.pallas_call(
        join_kernel,
        out_shape=jax.ShapeDtypeStruct((4, 16, W_COLS), jnp.bfloat16),
        in_specs=[pl.BlockSpec(memory_space=pltpu.SMEM), vmem, vmem],
        out_specs=vmem,
        name="join_cores",
    )(c.reshape(1), mine, theirs)


N_W, N_L, N_R = 9, 4, 4


def main_kernel(place_ref, *refs):
    w_refs, refs = refs[:N_W], refs[N_W:]
    a_refs, b_refs, r_refs = refs[:N_L], refs[N_L : 2 * N_L], refs[2 * N_L : 2 * N_L + N_R]
    ex_ref, w, lat, rs, kn, kr, qn, qr, bias, sems = refs[2 * N_L + N_R :]
    x, z, c, y = (place_ref[n] for n in range(4))
    xo = lax.rem(z, 2) + 2 * c
    met = (0, 1 + 2 * c, 3 - 2 * c, 2)
    index = [lax.rem((x ^ m) - xo + 4, 4) for m in met]
    slots = [lax.rem(x - (y ^ m) + 4, 4) for m in met]
    count = [0]

    def fetch(src, dst):
        copy = pltpu.make_async_copy(src, dst, sems.at[count[0]])
        count[0] += 1
        copy.start()
        return copy

    sign = 2 * c - 1
    early = [fetch(r_refs[d].at[:, pl.ds(640, 512)], rs.at[d]) for d in range(4)]
    late = []
    for n in range(N_W):
        step = (n + 1) // 2
        towards = sign if n % 2 else -sign
        rows = pl.ds(pl.multiple_of(lax.rem(z + towards * step + 8, 8) * 16, 16), 16)
        if step < 4:
            late.append(fetch(w_refs[n], w.at[:, rows, :]))
        else:
            half = pl.ds(2 * c, 2) if n % 2 else pl.ds(2 - 2 * c, 2)
            late.append(fetch(w_refs[n], w.at[half, rows, :]))
    low, high = pl.ds(0, 128), pl.ds(128, 128)
    for d in range(4):
        late.append(fetch(a_refs[d], lat.at[d, :, low, :]))
        late.append(fetch(b_refs[d], lat.at[:, d, high, :]))

    for copy in early:
        copy.wait()
    lane = lax.broadcasted_iota(jnp.int32, (128, 128), 1)
    seg_rows = []
    for d in range(4):
        seg_row = []
        for n in range(4):
            at = d + 4 * (n % 2)
            rows = pl.ds((n // 2) * 128, 128)
            part = rs[d, :, n * 128 : n * 128 + 128].astype(jnp.float32)
            kr[0, at, rows, :] = jnp.where(lane < 64, part, 0.0).astype(jnp.bfloat16)
            turned = pltpu.roll(part, 64, 1)
            kr[1, at, rows, :] = jnp.where(lane >= 64, turned, 0.0).astype(jnp.bfloat16)
            kr[2, at, rows, :] = turned.astype(jnp.bfloat16)
            if n % 2 == 0:
                seg_row.append(jnp.transpose(part)[64:65, :])
        seg_rows.append(jnp.concatenate(seg_row, axis=1))
    k_iota = lax.broadcasted_iota(jnp.int32, (BLK, BLK), 0)
    q_iota = lax.broadcasted_iota(jnp.int32, (BLK, BLK), 1)
    which = []
    for d in range(4):
        for f in range(4):
            at = jnp.where(index[f] > index[d], f + 4, f)
            which.append(at)
            seg_k = kr[2, at, :, 0:1].astype(jnp.float32)
            allowed = seg_k == seg_rows[d]
            if d == f:
                allowed = allowed & (k_iota <= q_iota)
            bias[d, f] = jnp.where(allowed, 0.0, NEG)

    for copy in late:
        copy.wait()
    k_scale = 1.0 / math.sqrt(KVLORA)
    wk = jnp.concatenate([w[slot, :, 3 * Q_COLS :] for slot in slots], axis=0)
    for b in range(8):
        at = 384 + 128 * (b // 4)
        kv = jnp.concatenate([lat[b % 4, e, :, at : at + 128] for e in range(4)], axis=1)
        kn[b] = (jnp.dot(kv, wk, preferred_element_type=jnp.float32) * k_scale).astype(jnp.bfloat16)
    q_scale = 1.0 / math.sqrt(QLORA)
    for out, at, columns in ((qn, 0, 512), (qn, 512, 512), (qr, 1024, 512)):
        wq = [
            w[slot, :, t * Q_COLS + at : t * Q_COLS + at + columns]
            for slot in slots
            for t in range(3)
        ]
        wq = jnp.concatenate(wq, axis=0)
        for d in range(4):
            ql = jnp.concatenate([lat[d, e, :, :384] for e in range(4)], axis=1)
            to = at % 1024
            out[d, :, to : to + columns] = (
                jnp.dot(ql, wq, preferred_element_type=jnp.float32) * q_scale
            ).astype(jnp.bfloat16)

    score_scale = 1.0 / math.sqrt(D_NOPE + D_ROPE)
    for h in range(HEADS):
        best_h = None
        for d in range(4):
            pair = (h // 2) * 128
            query = jnp.concatenate(
                [qn[d, :, h * 128 : h * 128 + 128], qr[d, :, pair : pair + 128]], axis=1
            )
            best = None
            for f in range(4):
                at = which[d * 4 + f]
                keys = jnp.concatenate([kn[at, :, h * 128 : h * 128 + 128], kr[h % 2, at]], axis=1)
                s = lax.dot_general(
                    keys, query, (((1,), (1,)), ((), ())), preferred_element_type=jnp.float32
                )
                s = jnp.max((s + bias[d, f]).reshape(BLK // 8, 8, BLK), axis=0)
                best = s if best is None else jnp.maximum(best, s)
            row = jnp.max(best, axis=0, keepdims=True) * score_scale
            ex_ref[4 * xo + index[d], h : h + 1, 0:BLK] = row
            best_h = row if best_h is None else jnp.maximum(best_h, row)
        top = jnp.max(best_h, axis=1, keepdims=True)
        ex_ref[0, h : h + 1, BLK:] = jnp.broadcast_to(top, (1, 128))
    tops = ex_ref[0, :, BLK:]
    for n in range(1, 16):
        ex_ref[n, :, BLK:] = tops


def main(place, w, a, b, r):
    vmem = pl.BlockSpec(memory_space=pltpu.VMEM)
    bf16, f32 = jnp.bfloat16, jnp.float32
    return pl.pallas_call(
        main_kernel,
        out_shape=jax.ShapeDtypeStruct((16, HEADS, BLK + 128), f32),
        in_specs=[pl.BlockSpec(memory_space=pltpu.SMEM)]
        + [pl.BlockSpec(memory_space=pl.ANY)] * (N_W + 2 * N_L + N_R),
        out_specs=vmem,
        scratch_shapes=[
            pltpu.VMEM((4, 128, W_COLS), bf16),
            pltpu.VMEM((4, 4, BLK, 640), bf16),
            pltpu.VMEM((4, 128, 512), bf16),
            pltpu.VMEM((8, BLK, 1024), bf16),
            pltpu.VMEM((3, 8, BLK, 128), bf16),
            pltpu.VMEM((4, BLK, 1024), bf16),
            pltpu.VMEM((4, BLK, 512), bf16),
            pltpu.VMEM((4, 4, BLK, BLK), f32),
            pltpu.SemaphoreType.DMA((N_W + 2 * N_L + N_R,)),
        ],
        compiler_params=pltpu.CompilerParams(vmem_limit_bytes=48 * 2**20),
        cost_estimate=pl.CostEstimate(
            flops=2 * 2048 * 512 * 1024 + 2 * 1024 * 1536 * 1536 + 2 * 128 * 256**3,
            bytes_accessed=12 * 2**20,
            transcendentals=0,
        ),
        name="row_maxima",
    )(place, *w, *a, *b, *r)


def after(values, *others):
    return lax.optimization_barrier((values, others))[0]


def gathered(x, c, weights, latents):
    def along_z(value):
        return lax.ppermute(value, ("zh", "zl", "c"), Z_ROUTE)

    def along(value, axis, turn):
        if axis == "x":
            return lax.ppermute(value, ("x", "c"), X_ROUTES[turn])
        return lax.ppermute(value, ("c", "y"), Y_ROUTES[turn])

    own, halo = pack_latents(*latents)
    weights = after(weights, own)
    own = lax.ppermute(own, SEQ, OWN_ROUTE)
    halo = lax.ppermute(halo, SEQ, HALO_ROUTE)
    parts = pack_weights(x.reshape(1), *weights)
    moved = [parts[0], ring(parts[1], "x", 1), ring(parts[2], "x", 2), ring(parts[3], "x", -1)]
    mine = jnp.stack(moved)
    w0 = join(c, mine, ring(mine, "c", 1))
    w1 = along_z(w0)

    first = jnp.concatenate([own[:128, :512], halo[:128, :128]], axis=1)
    second = [
        own[128:, :512], halo[128:, :128],
        own[:128, 512:], halo[:128, 128:], own[128:, 512:], halo[128:, 128:],
    ]
    second = jnp.concatenate(second, axis=1)
    first, second = after((first, second), w0)
    y1, y2 = along(first, "y", 0), along(first, "y", 1)
    x1, x2 = along(second, "x", 0), along(second, "x", 1)
    y1, y2, x1, x2, w1 = after((y1, y2, x1, x2, w1))
    y3, x3 = along(y1, "y", 1), along(x1, "x", 1)
    w2, w1p = along_z(w1), ring(w1, "c", 1)
    y3, x3, w2 = after((y3, x3, w2), w1p)
    r = [second, x1, x2, x3]
    a = jnp.stack([first, y1, y2, y3])
    b = jnp.stack([v[:, :640] for v in r])
    a1, a2 = along(a, "x", 0), along(a, "x", 1)
    b1, b2 = along(b, "y", 0), along(b, "y", 1)
    w3 = along_z(w2)
    a1, a2, b1, b2, w2, w3 = after((a1, a2, b1, b2, w2, w3))
    a3, b3 = along(a1, "x", 1), along(b1, "y", 1)
    w4 = along_z(lax.dynamic_slice_in_dim(w3, 2 * c, 2, axis=0))
    w2p, w3p = ring(w2, "c", 1), ring(w3, "c", 1)
    w4p = ring(w4, "c", 1)
    return [w0, w1, w1p, w2, w2p, w3, w3p, w4, w4p], [a, a1, a2, a3], [b, b1, b2, b3], r


def local(q_latent, kv_latent, k_rope, segment_ids, w_q_nope, w_q_rope, w_kv_nope, threshold):
    x, zh, zl, c, y = (lax.axis_index(a).astype(jnp.int32) for a in ("x", "zh", "zl", "c", "y"))
    weights = (w_q_nope, w_q_rope, w_kv_nope)
    latents = (q_latent, kv_latent, k_rope, segment_ids)
    w, a, b, r = gathered(x, c, weights, latents)
    out = main(jnp.stack([x, 2 * zh + zl, c, y]), w, a, b, r)

    got = lax.all_to_all(out, ("x", "zl", "c"), 0, 0, tiled=True)
    got = got.reshape(4, 4, HEADS, BLK + 128)
    top = jnp.max(got[..., BLK:], axis=1).reshape(4 * HEADS, 128)
    tops = lax.all_to_all(jnp.broadcast_to(top[None], (4, 32, 128)), "zh", 0, 0, tiled=True)
    head_max = jnp.max(tops, axis=0)[:, 0]
    sent_from = 2 * lax.rem(x, 2) + x // 2
    rows = lax.dynamic_slice_in_dim(got[..., :BLK], sent_from, 1, axis=1)
    row_max = rows.reshape(4 * HEADS, BLK).T

    clip = threshold[0] / jnp.maximum(head_max, threshold[0])
    root = jnp.sqrt(clip)
    new_q_nope = (w_q_nope.astype(jnp.float32) * jnp.repeat(root, D_NOPE)[None, :]).astype(
        jnp.bfloat16
    )
    new_q_rope = (w_q_rope.astype(jnp.float32) * jnp.repeat(clip, D_ROPE)[None, :]).astype(
        jnp.bfloat16
    )
    new_kv_nope = (w_kv_nope.astype(jnp.float32) * jnp.repeat(root, D_NOPE)[None, :]).astype(
        jnp.bfloat16
    )
    return (new_q_nope, new_q_rope, new_kv_nope, head_max, row_max)


def solution(mesh):
    fine = Mesh(mesh.devices.reshape(4, 4, 2, 2, 4), ("x", "zh", "zl", "c", "y"))
    in_specs = (
        P(SEQ, "y"),
        P(SEQ, "y"),
        P(SEQ, None),
        P(SEQ),
        P(SEQ, "y"),
        P(SEQ, "y"),
        P(SEQ, "y"),
        P(),
    )
    out_specs = (P(SEQ, "y"), P(SEQ, "y"), P(SEQ, "y"), P("y"), P(SEQ, "y"))
    return jax.shard_map(local, mesh=fine, in_specs=in_specs, out_specs=out_specs, check_vma=False)
```

```python
import math

import jax
import jax.numpy as jnp
from jax import lax
from jax.experimental import pallas as pl
from jax.experimental.pallas import tpu as pltpu
from jax.sharding import Mesh
from jax.sharding import PartitionSpec as P

D_NOPE = 128
D_ROPE = 64
QLORA = 1536
KVLORA = 512
BLK = 256
HEADS = 8
Q_COLS = HEADS * (D_NOPE + D_ROPE)
W_COLS = 3 * Q_COLS + HEADS * D_NOPE
NEG = -1e30
SEQ = ("x", "zh", "zl", "c")


def place_of(block, shift=0):
    group, i = divmod(block, 4)
    group = (group + shift) % 16
    xo, zh = divmod(group, 4)
    x, z, c = (i + xo) % 4, zh * 2 + (xo & 1), xo >> 1
    return (x * 8 + z) * 2 + c


OWN_ROUTE = [(b, place_of(b)) for b in range(64)]
HALO_ROUTE = [(b, place_of(b, 1)) for b in range(60) if b % 4]
Z_ROUTE = [(z * 2 + c, (z + (-1 if c else 1)) % 8 * 2 + c) for z in range(8) for c in range(2)]

TURNS = ((1, 3), (3, 1))
X_ROUTES = [[(x * 2 + c, (x ^ TURNS[c][n]) * 2 + c) for x in range(4) for c in range(2)] for n in range(2)]
Y_ROUTES = [[(c * 4 + y, c * 4 + (y ^ TURNS[c][n])) for y in range(4) for c in range(2)] for n in range(2)]


def ring(value, axis, distance):
    n = lax.axis_size(axis)
    return lax.ppermute(value, axis, [(i, (i + distance) % n) for i in range(n)])


def pack_weights_kernel(x_ref, wn_ref, wr_ref, wk_ref, *out_refs):
    for d in range(4):
        to = lax.rem(x_ref[0] + d, 4)
        out = out_refs[d]
        for t in range(3):
            rows = pl.ds(t * 8, 8)
            at = t * Q_COLS
            out[:, at : at + 1024] = wn_ref[rows, pl.ds(pl.multiple_of(to * 1024, 1024), 1024)]
            out[:, at + 1024 : at + 1536] = wr_ref[rows, pl.ds(pl.multiple_of(to * 512, 512), 512)]
        out[:, 3 * Q_COLS :] = wk_ref[:, pl.ds(pl.multiple_of(to * 1024, 1024), 1024)]


def pack_weights(x, wn, wr, wk):
    vmem = pl.BlockSpec(memory_space=pltpu.VMEM)
    return pl.pallas_call(
        pack_weights_kernel,
        out_shape=[jax.ShapeDtypeStruct((8, W_COLS), jnp.bfloat16)] * 4,
        in_specs=[pl.BlockSpec(memory_space=pltpu.SMEM), vmem, vmem, vmem],
        out_specs=[vmem] * 4,
        name="pack_weights",
    )(x, wn, wr, wk)


def pack_latents_kernel(q_ref, kv_ref, rope_ref, seg_ref, own_ref, halo_ref):
    old = lax.broadcasted_iota(jnp.int32, (384, 384), 0)
    new = lax.broadcasted_iota(jnp.int32, (384, 384), 1)
    t, rest = new // 128, new % 128
    pick = old == (rest // 8) * 24 + t * 8 + rest % 8
    chosen = jnp.where(pick, 1.0, 0.0).astype(jnp.bfloat16)
    own_ref[:, :384] = jnp.dot(q_ref[...], chosen, preferred_element_type=jnp.float32).astype(
        jnp.bfloat16
    )
    kv = kv_ref[...]
    own_ref[:, 384:512] = kv
    halo_ref[:, :128] = kv
    seg = jnp.broadcast_to((seg_ref[...] + 1).astype(jnp.float32), (128, BLK))
    column = jnp.transpose(seg).astype(jnp.bfloat16)
    rope = jnp.transpose(rope_ref[...].astype(jnp.float32)).astype(jnp.bfloat16)
    for ref, at in ((own_ref, 512), (halo_ref, 128)):
        ref[:, at : at + 128] = column
        ref[:, at : at + 64] = rope


def pack_latents(q, kv, rope, seg):
    vmem = pl.BlockSpec(memory_space=pltpu.VMEM)
    return pl.pallas_call(
        pack_latents_kernel,
        out_shape=[
            jax.ShapeDtypeStruct((BLK, 640), jnp.bfloat16),
            jax.ShapeDtypeStruct((BLK, 256), jnp.bfloat16),
        ],
        in_specs=[vmem] * 4,
        out_specs=[vmem] * 2,
        name="pack_latents",
    )(q, kv, rope.T, seg.reshape(1, BLK))


def join_kernel(c_ref, mine_ref, theirs_ref, out_ref):
    for core in range(2):

        @pl.when(c_ref[0] == core)
        def _():
            out_ref[:, core * 8 : core * 8 + 8, :] = mine_ref[...]
            out_ref[:, 8 - core * 8 : 16 - core * 8, :] = theirs_ref[...]


def join(c, mine, theirs):
    vmem = pl.BlockSpec(memory_space=pltpu.VMEM)
    return pl.pallas_call(
        join_kernel,
        out_shape=jax.ShapeDtypeStruct((4, 16, W_COLS), jnp.bfloat16),
        in_specs=[pl.BlockSpec(memory_space=pltpu.SMEM), vmem, vmem],
        out_specs=vmem,
        name="join_cores",
    )(c.reshape(1), mine, theirs)


N_W, N_L, N_R = 8, 4, 4


def main_kernel(place_ref, *refs):
    w_refs, refs = refs[:N_W], refs[N_W:]
    a_refs, b_refs, r_refs = refs[:N_L], refs[N_L : 2 * N_L], refs[2 * N_L : 2 * N_L + N_R]
    ex_ref, w, lat, rs, kn, kr, qn, qr, bias, sems = refs[2 * N_L + N_R :]
    x, z, c, y = (place_ref[n] for n in range(4))
    xo = lax.rem(z, 2) + 2 * c
    met = (0, 1 + 2 * c, 3 - 2 * c, 2)
    index = [lax.rem((x ^ m) - xo + 4, 4) for m in met]
    slots = [lax.rem(x - (y ^ m) + 4, 4) for m in met]
    count = [0]

    def fetch(src, dst):
        copy = pltpu.make_async_copy(src, dst, sems.at[count[0]])
        count[0] += 1
        copy.start()
        return copy

    low, high = pl.ds(0, 128), pl.ds(128, 128)
    key_lanes, query_lanes = pl.ds(384, 256), pl.ds(0, 384)
    key_columns, query_columns = pl.ds(3 * Q_COLS, 1024), pl.ds(0, 3 * Q_COLS)

    def fetch_latents(lanes):
        copies = []
        for n in range(4):
            copies.append(fetch(a_refs[n].at[:, :, lanes], lat.at[n, :, low, lanes]))
            copies.append(fetch(b_refs[n].at[:, :, lanes], lat.at[:, n, high, lanes]))
        return copies

    sign = 2 * c - 1

    def fetch_weights(columns):
        copies = []
        for n in range(N_W):
            step = (n + 1) // 2
            towards = sign if n % 2 else -sign
            rows = pl.ds(pl.multiple_of(lax.rem(z + towards * step + 8, 8) * 16, 16), 16)
            copies.append(fetch(w_refs[n].at[:, :, columns], w.at[:, rows, columns]))
        return copies

    early = [fetch(r_refs[d].at[:, pl.ds(640, 512)], rs.at[d]) for d in range(4)]
    middle = fetch_weights(key_columns) + fetch_latents(key_lanes)
    late = fetch_weights(query_columns) + fetch_latents(query_lanes)

    for copy in early:
        copy.wait()
    lane = lax.broadcasted_iota(jnp.int32, (128, 128), 1)
    seg_rows = []
    for d in range(4):
        seg_row = []
        for n in range(4):
            at = d + 4 * (n % 2)
            rows = pl.ds((n // 2) * 128, 128)
            part = rs[d, :, n * 128 : n * 128 + 128].astype(jnp.float32)
            kr[0, at, rows, :] = jnp.where(lane < 64, part, 0.0).astype(jnp.bfloat16)
            turned = pltpu.roll(part, 64, 1)
            kr[1, at, rows, :] = jnp.where(lane >= 64, turned, 0.0).astype(jnp.bfloat16)
            kr[2, at, rows, :] = turned.astype(jnp.bfloat16)
            if n % 2 == 0:
                seg_row.append(jnp.transpose(part)[64:65, :])
        seg_rows.append(jnp.concatenate(seg_row, axis=1))
    k_iota = lax.broadcasted_iota(jnp.int32, (BLK, BLK), 0)
    q_iota = lax.broadcasted_iota(jnp.int32, (BLK, BLK), 1)
    which = []
    for d in range(4):
        for f in range(4):
            at = jnp.where(index[f] > index[d], f + 4, f)
            which.append(at)
            seg_k = kr[2, at, :, 0:1].astype(jnp.float32)
            allowed = seg_k == seg_rows[d]
            if d == f:
                allowed = allowed & (k_iota <= q_iota)
            bias[d, f] = jnp.where(allowed, 0.0, NEG)

    for copy in middle:
        copy.wait()
    k_scale = 1.0 / math.sqrt(KVLORA)
    wk = jnp.concatenate([w[slot, :, 3 * Q_COLS :] for slot in slots], axis=0)
    for b in range(8):
        at = 384 + 128 * (b // 4)
        kv = jnp.concatenate([lat[b % 4, e, :, at : at + 128] for e in range(4)], axis=1)
        kn[b] = (jnp.dot(kv, wk, preferred_element_type=jnp.float32) * k_scale).astype(jnp.bfloat16)
    for copy in late:
        copy.wait()
    q_scale = 1.0 / math.sqrt(QLORA)
    for out, at, columns in ((qn, 0, 512), (qn, 512, 512), (qr, 1024, 512)):
        wq = [
            w[slot, :, t * Q_COLS + at : t * Q_COLS + at + columns]
            for slot in slots
            for t in range(3)
        ]
        wq = jnp.concatenate(wq, axis=0)
        for d in range(4):
            ql = jnp.concatenate([lat[d, e, :, :384] for e in range(4)], axis=1)
            to = at % 1024
            out[d, :, to : to + columns] = (
                jnp.dot(ql, wq, preferred_element_type=jnp.float32) * q_scale
            ).astype(jnp.bfloat16)

    score_scale = 1.0 / math.sqrt(D_NOPE + D_ROPE)
    for h in range(HEADS):
        best_h = None
        for d in range(4):
            pair = (h // 2) * 128
            query = jnp.concatenate(
                [qn[d, :, h * 128 : h * 128 + 128], qr[d, :, pair : pair + 128]], axis=1
            )
            best = None
            for f in range(4):
                at = which[d * 4 + f]
                keys = jnp.concatenate([kn[at, :, h * 128 : h * 128 + 128], kr[h % 2, at]], axis=1)
                s = lax.dot_general(
                    keys, query, (((1,), (1,)), ((), ())), preferred_element_type=jnp.float32
                )
                s = jnp.max((s + bias[d, f]).reshape(BLK // 8, 8, BLK), axis=0)
                best = s if best is None else jnp.maximum(best, s)
            row = jnp.max(best, axis=0, keepdims=True) * score_scale
            ex_ref[4 * xo + index[d], h : h + 1, 0:BLK] = row
            best_h = row if best_h is None else jnp.maximum(best_h, row)
        top = jnp.max(best_h, axis=1, keepdims=True)
        ex_ref[0, h : h + 1, BLK:] = jnp.broadcast_to(top, (1, 128))
    tops = ex_ref[0, :, BLK:]
    for n in range(1, 16):
        ex_ref[n, :, BLK:] = tops


def main(place, w, a, b, r):
    vmem = pl.BlockSpec(memory_space=pltpu.VMEM)
    bf16, f32 = jnp.bfloat16, jnp.float32
    return pl.pallas_call(
        main_kernel,
        out_shape=jax.ShapeDtypeStruct((16, HEADS, BLK + 128), f32),
        in_specs=[pl.BlockSpec(memory_space=pltpu.SMEM)]
        + [pl.BlockSpec(memory_space=pl.ANY)] * (N_W + 2 * N_L + N_R),
        out_specs=vmem,
        scratch_shapes=[
            pltpu.VMEM((4, 128, W_COLS), bf16),
            pltpu.VMEM((4, 4, BLK, 640), bf16),
            pltpu.VMEM((4, 128, 512), bf16),
            pltpu.VMEM((8, BLK, 1024), bf16),
            pltpu.VMEM((3, 8, BLK, 128), bf16),
            pltpu.VMEM((4, BLK, 1024), bf16),
            pltpu.VMEM((4, BLK, 512), bf16),
            pltpu.VMEM((4, 4, BLK, BLK), f32),
            pltpu.SemaphoreType.DMA((2 * N_W + 4 * N_L + N_R,)),
        ],
        compiler_params=pltpu.CompilerParams(vmem_limit_bytes=48 * 2**20),
        cost_estimate=pl.CostEstimate(
            flops=2 * 2048 * 512 * 1024 + 2 * 1024 * 1536 * 1536 + 2 * 128 * 256**3,
            bytes_accessed=12 * 2**20,
            transcendentals=0,
        ),
        name="row_maxima",
    )(place, *(pltpu.with_memory_space_constraint(v, pltpu.HBM) for v in (*w, *a, *b, *r)))


def after(values, *others):
    return lax.optimization_barrier((values, others))[0]


def gathered(x, c, weights, latents):
    def along_z(value):
        return lax.ppermute(value, ("zh", "zl", "c"), Z_ROUTE)

    def along(value, axis, turn):
        if axis == "x":
            return lax.ppermute(value, ("x", "c"), X_ROUTES[turn])
        return lax.ppermute(value, ("c", "y"), Y_ROUTES[turn])

    own, halo = pack_latents(*latents)
    weights = after(weights, own)
    halo = lax.ppermute(halo, SEQ, HALO_ROUTE)
    own = lax.ppermute(own, SEQ, OWN_ROUTE)
    parts = pack_weights(x.reshape(1), *weights)
    moved = [parts[0], ring(parts[1], "x", 1), ring(parts[2], "x", 2), ring(parts[3], "x", -1)]
    mine = jnp.stack(moved)
    w0 = join(c, mine, ring(mine, "c", 1))
    w1 = along_z(w0)
    first = jnp.concatenate([own[:128, :512], halo[:128, :128]], axis=1)
    second = [
        own[128:, :512], halo[128:, :128],
        own[:128, 512:], halo[:128, 128:], own[128:, 512:], halo[128:, 128:],
    ]
    second = jnp.concatenate(second, axis=1)
    first, second = after((first, second), w0)
    y1, y2 = along(first, "y", 0), along(first, "y", 1)
    x1, x2 = along(second, "x", 0), along(second, "x", 1)
    y1, y2, x1, x2, w1 = after((y1, y2, x1, x2, w1))
    y3, x3 = along(y1, "y", 1), along(x1, "x", 1)
    w2, w1p = along_z(w1), ring(w1, "c", 1)
    y3, x3, w2 = after((y3, x3, w2), w1p)
    r = [second, x1, x2, x3]
    a = jnp.stack([first, y1, y2, y3])
    b = jnp.stack([v[:, :640] for v in r])
    a1, a2 = along(a, "x", 0), along(a, "x", 1)
    b1, b2 = along(b, "y", 0), along(b, "y", 1)
    w3 = along_z(w2)
    a1, a2, b1, b2, w2, w3 = after((a1, a2, b1, b2, w2, w3))
    a3, b3 = along(a1, "x", 1), along(b1, "y", 1)
    w4, w2p, w3p = along_z(w3), ring(w2, "c", 1), ring(w3, "c", 1)
    return [w0, w1, w1p, w2, w2p, w3, w3p, w4], [a, a1, a2, a3], [b, b1, b2, b3], r


def scale_kernel(threshold_ref, tops_ref, wn_ref, wr_ref, wk_ref, nn_ref, nr_ref, nk_ref, hm_ref):
    top = tops_ref[0]
    for n in range(1, 4):
        top = jnp.maximum(top, tops_ref[n])
    threshold = jnp.full(top.shape, threshold_ref[0], jnp.float32)
    clip = threshold / jnp.maximum(top, threshold)
    root = jnp.sqrt(clip)
    for h in range(32):
        at = slice(h * 128, h * 128 + 128)
        by = root[h : h + 1, :]
        nn_ref[:, at] = (wn_ref[:, at].astype(jnp.float32) * by).astype(jnp.bfloat16)
        nk_ref[:, at] = (wk_ref[:, at].astype(jnp.float32) * by).astype(jnp.bfloat16)
    lane = lax.broadcasted_iota(jnp.int32, (1, 128), 1)
    for p in range(16):
        at = slice(p * 128, p * 128 + 128)
        by = jnp.where(lane < 64, clip[2 * p : 2 * p + 1, :], clip[2 * p + 1 : 2 * p + 2, :])
        nr_ref[:, at] = (wr_ref[:, at].astype(jnp.float32) * by).astype(jnp.bfloat16)
    row = lax.broadcasted_iota(jnp.int32, (32, 128), 0)
    column = lax.broadcasted_iota(jnp.int32, (32, 128), 1)
    line = jnp.sum(jnp.where(row == column, top, 0.0), axis=0, keepdims=True)
    hm_ref[...] = line[:, :32]


def scaled(threshold, tops, wn, wr, wk):
    vmem = pl.BlockSpec(memory_space=pltpu.VMEM)
    return pl.pallas_call(
        scale_kernel,
        out_shape=[jax.ShapeDtypeStruct(v.shape, v.dtype) for v in (wn, wr, wk)]
        + [jax.ShapeDtypeStruct((1, 32), jnp.float32)],
        in_specs=[pl.BlockSpec(memory_space=pltpu.SMEM)] + [vmem] * 4,
        out_specs=[vmem] * 4,
        name="scaled_weights",
    )(threshold, tops, wn, wr, wk)


def local(q_latent, kv_latent, k_rope, segment_ids, w_q_nope, w_q_rope, w_kv_nope, threshold):
    x, zh, zl, c, y = (lax.axis_index(a).astype(jnp.int32) for a in ("x", "zh", "zl", "c", "y"))
    weights = (w_q_nope, w_q_rope, w_kv_nope)
    latents = (q_latent, kv_latent, k_rope, segment_ids)
    w, a, b, r = gathered(x, c, weights, latents)
    out = main(jnp.stack([x, 2 * zh + zl, c, y]), w, a, b, r)

    got = lax.all_to_all(out, ("x", "zl", "c"), 0, 0, tiled=True)
    got = got.reshape(4, 4, HEADS, BLK + 128)
    top = jnp.max(got[..., BLK:], axis=1).reshape(4 * HEADS, 128)
    tops = lax.all_to_all(jnp.broadcast_to(top[None], (4, 32, 128)), "zh", 0, 0, tiled=True)
    new_q_nope, new_q_rope, new_kv_nope, head_max = scaled(threshold, tops, *weights)
    sent_from = 2 * lax.rem(x, 2) + x // 2
    rows = lax.dynamic_slice_in_dim(got[..., :BLK], sent_from, 1, axis=1)
    row_max = rows.reshape(4 * HEADS, BLK).T

    return (new_q_nope, new_q_rope, new_kv_nope, head_max.reshape(32), row_max)


def solution(mesh):
    fine = Mesh(mesh.devices.reshape(4, 4, 2, 2, 4), ("x", "zh", "zl", "c", "y"))
    in_specs = (
        P(SEQ, "y"),
        P(SEQ, "y"),
        P(SEQ, None),
        P(SEQ),
        P(SEQ, "y"),
        P(SEQ, "y"),
        P(SEQ, "y"),
        P(),
    )
    out_specs = (P(SEQ, "y"), P(SEQ, "y"), P(SEQ, "y"), P("y"), P(SEQ, "y"))
    return jax.shard_map(local, mesh=fine, in_specs=in_specs, out_specs=out_specs, check_vma=False)
```

```python
import math

import jax
import jax.numpy as jnp
from jax import lax
from jax.experimental import pallas as pl
from jax.experimental.pallas import tpu as pltpu
from jax.sharding import Mesh
from jax.sharding import PartitionSpec as P

D_NOPE = 128
D_ROPE = 64
QLORA = 1536
KVLORA = 512
BLK = 256
HEADS = 8
Q_COLS = HEADS * (D_NOPE + D_ROPE)
W_COLS = 3 * Q_COLS + HEADS * D_NOPE
NEG = -1e30
SEQ = ("x", "zh", "zl", "c")


def place_of(block, shift=0):
    group, i = divmod(block, 4)
    group = (group + shift) % 16
    xo, zh = divmod(group, 4)
    x, z, c = (i + xo) % 4, zh * 2 + (xo & 1), xo >> 1
    return (x * 8 + z) * 2 + c


OWN_ROUTE = [(b, place_of(b)) for b in range(64)]
HALO_ROUTE = [(b, place_of(b, 1)) for b in range(60) if b % 4]
Z_ROUTE = [(z * 2 + c, (z + (-1 if c else 1)) % 8 * 2 + c) for z in range(8) for c in range(2)]

TURNS = ((1, 3), (3, 1))
X_ROUTES = [[(x * 2 + c, (x ^ TURNS[c][n]) * 2 + c) for x in range(4) for c in range(2)] for n in range(2)]
Y_ROUTES = [[(c * 4 + y, c * 4 + (y ^ TURNS[c][n])) for y in range(4) for c in range(2)] for n in range(2)]


def ring(value, axis, distance):
    n = lax.axis_size(axis)
    return lax.ppermute(value, axis, [(i, (i + distance) % n) for i in range(n)])


def pack_weights_kernel(x_ref, wn_ref, wr_ref, wk_ref, *out_refs):
    for d in range(4):
        to = lax.rem(x_ref[0] + d, 4)
        out = out_refs[d]
        for t in range(3):
            rows = pl.ds(t * 8, 8)
            at = t * Q_COLS
            out[:, at : at + 1024] = wn_ref[rows, pl.ds(pl.multiple_of(to * 1024, 1024), 1024)]
            out[:, at + 1024 : at + 1536] = wr_ref[rows, pl.ds(pl.multiple_of(to * 512, 512), 512)]
        out[:, 3 * Q_COLS :] = wk_ref[:, pl.ds(pl.multiple_of(to * 1024, 1024), 1024)]


def pack_weights(x, wn, wr, wk):
    vmem = pl.BlockSpec(memory_space=pltpu.VMEM)
    return pl.pallas_call(
        pack_weights_kernel,
        out_shape=[jax.ShapeDtypeStruct((8, W_COLS), jnp.bfloat16)] * 4,
        in_specs=[pl.BlockSpec(memory_space=pltpu.SMEM), vmem, vmem, vmem],
        out_specs=[vmem] * 4,
        name="pack_weights",
    )(x, wn, wr, wk)


def pack_latents_kernel(q_ref, kv_ref, rope_ref, seg_ref, own_ref, halo_ref):
    old = lax.broadcasted_iota(jnp.int32, (384, 384), 0)
    new = lax.broadcasted_iota(jnp.int32, (384, 384), 1)
    t, rest = new // 128, new % 128
    pick = old == (rest // 8) * 24 + t * 8 + rest % 8
    chosen = jnp.where(pick, 1.0, 0.0).astype(jnp.bfloat16)
    own_ref[:, :384] = jnp.dot(q_ref[...], chosen, preferred_element_type=jnp.float32).astype(
        jnp.bfloat16
    )
    kv = kv_ref[...]
    own_ref[:, 384:512] = kv
    halo_ref[:, :128] = kv
    seg = jnp.broadcast_to((seg_ref[...] + 1).astype(jnp.float32), (128, BLK))
    column = jnp.transpose(seg).astype(jnp.bfloat16)
    rope = jnp.transpose(rope_ref[...].astype(jnp.float32)).astype(jnp.bfloat16)
    for ref, at in ((own_ref, 512), (halo_ref, 128)):
        ref[:, at : at + 128] = column
        ref[:, at : at + 64] = rope


def pack_latents(q, kv, rope, seg):
    vmem = pl.BlockSpec(memory_space=pltpu.VMEM)
    return pl.pallas_call(
        pack_latents_kernel,
        out_shape=[
            jax.ShapeDtypeStruct((BLK, 640), jnp.bfloat16),
            jax.ShapeDtypeStruct((BLK, 256), jnp.bfloat16),
        ],
        in_specs=[vmem] * 4,
        out_specs=[vmem] * 2,
        name="pack_latents",
    )(q, kv, rope.T, seg.reshape(1, BLK))


def join_kernel(c_ref, mine_ref, theirs_ref, out_ref):
    for core in range(2):

        @pl.when(c_ref[0] == core)
        def _():
            out_ref[:, core * 8 : core * 8 + 8, :] = mine_ref[...]
            out_ref[:, 8 - core * 8 : 16 - core * 8, :] = theirs_ref[...]


def join(c, mine, theirs):
    vmem = pl.BlockSpec(memory_space=pltpu.VMEM)
    return pl.pallas_call(
        join_kernel,
        out_shape=jax.ShapeDtypeStruct((4, 16, W_COLS), jnp.bfloat16),
        in_specs=[pl.BlockSpec(memory_space=pltpu.SMEM), vmem, vmem],
        out_specs=vmem,
        name="join_cores",
    )(c.reshape(1), mine, theirs)


N_W, N_L, N_R = 9, 4, 4


def main_kernel(place_ref, *refs):
    w_refs, refs = refs[:N_W], refs[N_W:]
    a_refs, b_refs, r_refs = refs[:N_L], refs[N_L : 2 * N_L], refs[2 * N_L : 2 * N_L + N_R]
    ex_ref, w, lat, rs, kn, kr, qn, qr, bias, sems = refs[2 * N_L + N_R :]
    x, z, c, y = (place_ref[n] for n in range(4))
    xo = lax.rem(z, 2) + 2 * c
    met = (0, 1 + 2 * c, 3 - 2 * c, 2)
    index = [lax.rem((x ^ m) - xo + 4, 4) for m in met]
    slots = [lax.rem(x - (y ^ m) + 4, 4) for m in met]
    count = [0]

    def fetch(src, dst):
        copy = pltpu.make_async_copy(src, dst, sems.at[count[0]])
        count[0] += 1
        copy.start()
        return copy

    low, high = pl.ds(0, 128), pl.ds(128, 128)
    key_lanes, query_lanes = pl.ds(384, 256), pl.ds(0, 384)
    key_columns, query_columns = pl.ds(3 * Q_COLS, 1024), pl.ds(0, 3 * Q_COLS)

    def fetch_latents(lanes):
        copies = []
        for n in range(4):
            copies.append(fetch(a_refs[n].at[:, :, lanes], lat.at[n, :, low, lanes]))
            copies.append(fetch(b_refs[n].at[:, :, lanes], lat.at[:, n, high, lanes]))
        return copies

    sign = 2 * c - 1

    def fetch_weights(columns):
        copies = []
        for n in range(N_W):
            step = (n + 1) // 2
            towards = sign if n % 2 else -sign
            rows = pl.ds(pl.multiple_of(lax.rem(z + towards * step + 8, 8) * 16, 16), 16)
            half = pl.ds(0, 4) if step < 4 else pl.ds(2 * c if n % 2 else 2 - 2 * c, 2)
            copies.append(fetch(w_refs[n].at[:, :, columns], w.at[half, rows, columns]))
        return copies

    early = [fetch(r_refs[d].at[:, pl.ds(640, 512)], rs.at[d]) for d in range(4)]
    middle = fetch_weights(key_columns) + fetch_latents(key_lanes)
    late = fetch_weights(query_columns) + fetch_latents(query_lanes)

    for copy in early:
        copy.wait()
    lane = lax.broadcasted_iota(jnp.int32, (128, 128), 1)
    seg_rows = []
    for d in range(4):
        seg_row = []
        for n in range(4):
            at = d + 4 * (n % 2)
            rows = pl.ds((n // 2) * 128, 128)
            part = rs[d, :, n * 128 : n * 128 + 128].astype(jnp.float32)
            kr[0, at, rows, :] = jnp.where(lane < 64, part, 0.0).astype(jnp.bfloat16)
            turned = pltpu.roll(part, 64, 1)
            kr[1, at, rows, :] = jnp.where(lane >= 64, turned, 0.0).astype(jnp.bfloat16)
            kr[2, at, rows, :] = turned.astype(jnp.bfloat16)
            if n % 2 == 0:
                seg_row.append(jnp.transpose(part)[64:65, :])
        seg_rows.append(jnp.concatenate(seg_row, axis=1))
    k_iota = lax.broadcasted_iota(jnp.int32, (BLK, BLK), 0)
    q_iota = lax.broadcasted_iota(jnp.int32, (BLK, BLK), 1)
    which = []
    for d in range(4):
        for f in range(4):
            at = jnp.where(index[f] > index[d], f + 4, f)
            which.append(at)
            seg_k = kr[2, at, :, 0:1].astype(jnp.float32)
            allowed = seg_k == seg_rows[d]
            if d == f:
                allowed = allowed & (k_iota <= q_iota)
            bias[d, f] = jnp.where(allowed, 0.0, NEG)

    for copy in middle:
        copy.wait()
    k_scale = 1.0 / math.sqrt(KVLORA)
    wk = jnp.concatenate([w[slot, :, 3 * Q_COLS :] for slot in slots], axis=0)
    for b in range(8):
        at = 384 + 128 * (b // 4)
        kv = jnp.concatenate([lat[b % 4, e, :, at : at + 128] for e in range(4)], axis=1)
        kn[b] = (jnp.dot(kv, wk, preferred_element_type=jnp.float32) * k_scale).astype(jnp.bfloat16)
    for copy in late:
        copy.wait()
    q_scale = 1.0 / math.sqrt(QLORA)
    for out, at, columns in ((qn, 0, 512), (qn, 512, 512), (qr, 1024, 512)):
        wq = [
            w[slot, :, t * Q_COLS + at : t * Q_COLS + at + columns]
            for slot in slots
            for t in range(3)
        ]
        wq = jnp.concatenate(wq, axis=0)
        for d in range(4):
            ql = jnp.concatenate([lat[d, e, :, :384] for e in range(4)], axis=1)
            to = at % 1024
            out[d, :, to : to + columns] = (
                jnp.dot(ql, wq, preferred_element_type=jnp.float32) * q_scale
            ).astype(jnp.bfloat16)

    score_scale = 1.0 / math.sqrt(D_NOPE + D_ROPE)
    for h in range(HEADS):
        best_h = None
        for d in range(4):
            pair = (h // 2) * 128
            query = jnp.concatenate(
                [qn[d, :, h * 128 : h * 128 + 128], qr[d, :, pair : pair + 128]], axis=1
            )
            best = None
            for f in range(4):
                at = which[d * 4 + f]
                keys = jnp.concatenate([kn[at, :, h * 128 : h * 128 + 128], kr[h % 2, at]], axis=1)
                s = lax.dot_general(
                    keys, query, (((1,), (1,)), ((), ())), preferred_element_type=jnp.float32
                )
                s = jnp.max((s + bias[d, f]).reshape(BLK // 8, 8, BLK), axis=0)
                best = s if best is None else jnp.maximum(best, s)
            row = jnp.max(best, axis=0, keepdims=True) * score_scale
            ex_ref[4 * xo + index[d], h : h + 1, 0:BLK] = row
            best_h = row if best_h is None else jnp.maximum(best_h, row)
        top = jnp.max(best_h, axis=1, keepdims=True)
        ex_ref[0, h : h + 1, BLK:] = jnp.broadcast_to(top, (1, 128))
    tops = ex_ref[0, :, BLK:]
    for n in range(1, 16):
        ex_ref[n, :, BLK:] = tops


def main(place, w, a, b, r):
    vmem = pl.BlockSpec(memory_space=pltpu.VMEM)
    bf16, f32 = jnp.bfloat16, jnp.float32
    return pl.pallas_call(
        main_kernel,
        out_shape=jax.ShapeDtypeStruct((16, HEADS, BLK + 128), f32),
        in_specs=[pl.BlockSpec(memory_space=pltpu.SMEM)]
        + [pl.BlockSpec(memory_space=pl.ANY)] * (N_W + 2 * N_L + N_R),
        out_specs=vmem,
        scratch_shapes=[
            pltpu.VMEM((4, 128, W_COLS), bf16),
            pltpu.VMEM((4, 4, BLK, 640), bf16),
            pltpu.VMEM((4, 128, 512), bf16),
            pltpu.VMEM((8, BLK, 1024), bf16),
            pltpu.VMEM((3, 8, BLK, 128), bf16),
            pltpu.VMEM((4, BLK, 1024), bf16),
            pltpu.VMEM((4, BLK, 512), bf16),
            pltpu.VMEM((4, 4, BLK, BLK), f32),
            pltpu.SemaphoreType.DMA((2 * N_W + 4 * N_L + N_R,)),
        ],
        compiler_params=pltpu.CompilerParams(vmem_limit_bytes=48 * 2**20),
        cost_estimate=pl.CostEstimate(
            flops=2 * 2048 * 512 * 1024 + 2 * 1024 * 1536 * 1536 + 2 * 128 * 256**3,
            bytes_accessed=12 * 2**20,
            transcendentals=0,
        ),
        name="row_maxima",
    )(place, *w, *a, *b, *r)


def after(values, *others):
    return lax.optimization_barrier((values, others))[0]


def gathered(x, c, weights, latents):
    def along_z(value):
        return lax.ppermute(value, ("zh", "zl", "c"), Z_ROUTE)

    def along(value, axis, turn):
        if axis == "x":
            return lax.ppermute(value, ("x", "c"), X_ROUTES[turn])
        return lax.ppermute(value, ("c", "y"), Y_ROUTES[turn])

    own, halo = pack_latents(*latents)
    weights = after(weights, own)
    halo = lax.ppermute(halo, SEQ, HALO_ROUTE)
    own = lax.ppermute(own, SEQ, OWN_ROUTE)
    parts = pack_weights(x.reshape(1), *weights)
    moved = [parts[0], ring(parts[1], "x", 1), ring(parts[2], "x", 2), ring(parts[3], "x", -1)]
    mine = jnp.stack(moved)
    w0 = join(c, mine, ring(mine, "c", 1))
    w1 = along_z(w0)
    first = jnp.concatenate([own[:128, :512], halo[:128, :128]], axis=1)
    second = [
        own[128:, :512], halo[128:, :128],
        own[:128, 512:], halo[:128, 128:], own[128:, 512:], halo[128:, 128:],
    ]
    second = jnp.concatenate(second, axis=1)
    first, second = after((first, second), w0)
    y1, y2 = along(first, "y", 0), along(first, "y", 1)
    x1, x2 = along(second, "x", 0), along(second, "x", 1)
    y1, y2, x1, x2, w1 = after((y1, y2, x1, x2, w1))
    y3, x3 = along(y1, "y", 1), along(x1, "x", 1)
    w2, w1p = along_z(w1), ring(w1, "c", 1)
    y3, x3, w2 = after((y3, x3, w2), w1p)
    r = [second, x1, x2, x3]
    a = jnp.stack([first, y1, y2, y3])
    b = jnp.stack([v[:, :640] for v in r])
    a1, a2 = along(a, "x", 0), along(a, "x", 1)
    b1, b2 = along(b, "y", 0), along(b, "y", 1)
    w3 = along_z(w2)
    a1, a2, b1, b2, w2, w3 = after((a1, a2, b1, b2, w2, w3))
    a3, b3 = along(a1, "x", 1), along(b1, "y", 1)
    w4 = along_z(lax.dynamic_slice_in_dim(w3, 2 * c, 2, axis=0))
    w2p, w3p = ring(w2, "c", 1), ring(w3, "c", 1)
    w4p = ring(w4, "c", 1)
    return [w0, w1, w1p, w2, w2p, w3, w3p, w4, w4p], [a, a1, a2, a3], [b, b1, b2, b3], r


def scale_kernel(threshold_ref, tops_ref, wn_ref, wr_ref, wk_ref, nn_ref, nr_ref, nk_ref, hm_ref):
    top = tops_ref[0]
    for n in range(1, 4):
        top = jnp.maximum(top, tops_ref[n])
    threshold = jnp.full(top.shape, threshold_ref[0], jnp.float32)
    clip = threshold / jnp.maximum(top, threshold)
    root = jnp.sqrt(clip)
    for h in range(32):
        at = slice(h * 128, h * 128 + 128)
        by = root[h : h + 1, :]
        nn_ref[:, at] = (wn_ref[:, at].astype(jnp.float32) * by).astype(jnp.bfloat16)
        nk_ref[:, at] = (wk_ref[:, at].astype(jnp.float32) * by).astype(jnp.bfloat16)
    lane = lax.broadcasted_iota(jnp.int32, (1, 128), 1)
    for p in range(16):
        at = slice(p * 128, p * 128 + 128)
        by = jnp.where(lane < 64, clip[2 * p : 2 * p + 1, :], clip[2 * p + 1 : 2 * p + 2, :])
        nr_ref[:, at] = (wr_ref[:, at].astype(jnp.float32) * by).astype(jnp.bfloat16)
    row = lax.broadcasted_iota(jnp.int32, (32, 128), 0)
    column = lax.broadcasted_iota(jnp.int32, (32, 128), 1)
    line = jnp.sum(jnp.where(row == column, top, 0.0), axis=0, keepdims=True)
    hm_ref[...] = line[:, :32]


def scaled(threshold, tops, wn, wr, wk):
    vmem = pl.BlockSpec(memory_space=pltpu.VMEM)
    return pl.pallas_call(
        scale_kernel,
        out_shape=[jax.ShapeDtypeStruct(v.shape, v.dtype) for v in (wn, wr, wk)]
        + [jax.ShapeDtypeStruct((1, 32), jnp.float32)],
        in_specs=[pl.BlockSpec(memory_space=pltpu.SMEM)] + [vmem] * 4,
        out_specs=[vmem] * 4,
        name="scaled_weights",
    )(threshold, tops, wn, wr, wk)


def local(q_latent, kv_latent, k_rope, segment_ids, w_q_nope, w_q_rope, w_kv_nope, threshold):
    x, zh, zl, c, y = (lax.axis_index(a).astype(jnp.int32) for a in ("x", "zh", "zl", "c", "y"))
    weights = (w_q_nope, w_q_rope, w_kv_nope)
    latents = (q_latent, kv_latent, k_rope, segment_ids)
    w, a, b, r = gathered(x, c, weights, latents)
    out = main(jnp.stack([x, 2 * zh + zl, c, y]), w, a, b, r)

    got = lax.all_to_all(out, ("x", "zl", "c"), 0, 0, tiled=True)
    got = got.reshape(4, 4, HEADS, BLK + 128)
    top = jnp.max(got[..., BLK:], axis=1).reshape(4 * HEADS, 128)
    tops = lax.all_to_all(jnp.broadcast_to(top[None], (4, 32, 128)), "zh", 0, 0, tiled=True)
    new_q_nope, new_q_rope, new_kv_nope, head_max = scaled(threshold, tops, *weights)
    sent_from = 2 * lax.rem(x, 2) + x // 2
    rows = lax.dynamic_slice_in_dim(got[..., :BLK], sent_from, 1, axis=1)
    row_max = rows.reshape(4 * HEADS, BLK).T

    return (new_q_nope, new_q_rope, new_kv_nope, head_max.reshape(32), row_max)


def solution(mesh):
    fine = Mesh(mesh.devices.reshape(4, 4, 2, 2, 4), ("x", "zh", "zl", "c", "y"))
    in_specs = (
        P(SEQ, "y"),
        P(SEQ, "y"),
        P(SEQ, None),
        P(SEQ),
        P(SEQ, "y"),
        P(SEQ, "y"),
        P(SEQ, "y"),
        P(),
    )
    out_specs = (P(SEQ, "y"), P(SEQ, "y"), P(SEQ, "y"), P("y"), P(SEQ, "y"))
    return jax.shard_map(local, mesh=fine, in_specs=in_specs, out_specs=out_specs, check_vma=False)
```
